256 devices in a mesh: ka: 32 (over x_hi, z, core), band: 8 (over x_lo, y).
Axes of the slice: x: 4 (x_hi: 2, x_lo: 2; x = x_hi * 2 + x_lo), y: 4, z: 8, core: 2. Of those that a mesh axis runs over, the one named last changes fastest.
Arguments:
- valence_orbitals: bfloat16 [32, 32, 64, 64, 128], P('ka', None, None, 'band'), may hold values from -6 to 6
- conduction_orbitals: bfloat16 [32, 1, 64, 64, 128], P(None, None, 'ka', 'band'), may hold values from -6 to 6
- valence_energy: float32 [32, 32], P('ka'), may hold values from -1.5 to -0.1
- conduction_energy: float32 [32, 1], replicated, may hold values from 0.1 to 1.5
- valence_select: int32 [32, 16], P('ka'), may hold values from 0 to 31, as said below
- shifted_index: int32 [32], replicated, may hold values from 0 to 31, each once
- wave_vectors: int32 [3, 2048], replicated, may hold values from -16 to 15
- frequency: float32 [1], replicated, may hold values from 0.3 to 1
Outputs:
- chi_zero: float32 [2, 2048, 2048], P(None, ('ka', 'band'))
The draws below stay inside these ranges and needn't reach their ends.
Inputs may be any that keep to these rules, and one draw needn't show every extreme that they name: `valence_select`: each row holds 16 different band numbers. `shifted_index`: every k point is the partner of exactly one k point.
All inputs are finite; a program needn't handle non-finite values.
Results may differ from the reference program's by a relative error of at most 0.025.
Values may be sent and summed in bfloat16 or wider, within the bound.
No kernel may reach another device: no remote copies, remote signals or barrier semaphores. Data moves between devices by JAX's collectives and lax.ppermute only.
A program may use at most 256 MiB of HBM per device.

```python
import jax
import jax.numpy as jnp
from jax import lax

GRID = 64
NG = 2048
NOCC = 16
NVAL = 32
NEMPTY = 1
NK = 32


def draw_valence_select(key, part):
    keys = jax.random.split(jax.random.fold_in(key, 17), NK)

    def one_row(subkey):
        return jax.random.permutation(subkey, NVAL)[:NOCC]
    return jax.vmap(one_row)(keys).astype(jnp.int32)


def set_ends(entries, rng, least, high):
    longest = entries.shape.index(max(entries.shape))
    spots = []
    for shift in (0, 1):
        where = [jax.random.randint(jax.random.fold_in(rng, axis), (), 0, length) for axis, length in enumerate(entries.shape)]
        where[longest] = (where[longest] + shift) % entries.shape[longest]
        spots.append(tuple(where))
    return entries.at[spots[0]].set(least).at[spots[1]].set(high)


def levels(rng, shape, pieces, smallest, largest):
    loudness, own = 1.0, jax.random.fold_in(rng, 6)
    for position, parts in pieces:
        steps = jnp.exp(jax.random.uniform(jax.random.fold_in(own, position), (parts,), jnp.float32, smallest / len(pieces), largest / len(pieces)))
        loudness = loudness * jnp.repeat(steps, shape[position] // parts).reshape([-1 if axis == position else 1 for axis in range(len(shape))])
    return loudness


def noise(own_key, extent, scale, limit, cuts=(), kind=jnp.bfloat16):
    result = scale * jax.random.normal(own_key, extent, jnp.float32)
    if cuts:
        result = result * levels(own_key, extent, cuts, -0.22, 0.18)
    return jnp.clip(result, -limit, limit).astype(kind)


def setup_inputs(seed: int = 0) -> dict:
    key_list = jax.random.split(jax.random.key(seed), 9)
    return {
        "valence_orbitals": noise(key_list[0], (NK, NVAL, GRID, GRID, 2 * GRID), 1.0, 6.0, ((0, 32), (3, 8))),
        "conduction_orbitals": noise(key_list[1], (NK, NEMPTY, GRID, GRID, 2 * GRID), 1.0, 6.0, ((2, 32), (3, 8))),
        "valence_energy": jnp.clip(-1.5 + 1.4 * jax.random.uniform(key_list[2], (NK, NVAL), jnp.float32) ** levels(key_list[2], (NK, NVAL), ((0, 32),), -0.2, 0.2), -1.5, -0.1),
        "conduction_energy": jnp.clip(jax.random.uniform(key_list[3], (NK, NEMPTY), jnp.float32, 0.1, 1.5), 0.1, 1.5),
        "valence_select": draw_valence_select(jax.random.fold_in(key_list[8], 71), 0),
        "shifted_index": jax.random.permutation(key_list[5], NK).astype(jnp.int32),
        "wave_vectors": set_ends(jax.random.randint(key_list[6], (3, NG), 0 - GRID // 4, GRID // 4), jax.random.fold_in(key_list[6], 1), 0 - GRID // 4, (GRID // 4) - 1).astype(jnp.int32),
        "frequency": jnp.clip(jax.random.uniform(key_list[7], (1,), jnp.float32, 0.3, 1.0), 0.3, 1.0),
    }


def reference(valence_orbitals, conduction_orbitals, valence_energy, conduction_energy, valence_select, shifted_index, wave_vectors, frequency):
    wrapped = jnp.mod(wave_vectors, GRID).astype(jnp.int32)
    norm_scale = float(GRID) ** -1.5

    def one_kpoint(running, kpoint):
        chosen = valence_select[kpoint]
        valence = jnp.take(valence_orbitals[kpoint], chosen, axis=0)
        partner = shifted_index[kpoint]
        conduction = conduction_orbitals[partner]
        energy_gap = jnp.take(valence_energy[kpoint], chosen)[:, None] - conduction_energy[partner][None, :]
        weight = 2.0 * energy_gap / (energy_gap * energy_gap + frequency[0] * frequency[0]) / (NK * NOCC)
        cond_real = conduction[..., :GRID].astype(jnp.float32)
        cond_imag = conduction[..., GRID:].astype(jnp.float32)

        def one_band(orbital):
            val_real = orbital[..., :GRID].astype(jnp.float32)
            val_imag = orbital[..., GRID:].astype(jnp.float32)
            pair_real = (val_real[None] * cond_real + val_imag[None] * cond_imag).astype(jnp.bfloat16)
            pair_imag = (val_real[None] * cond_imag - val_imag[None] * cond_real).astype(jnp.bfloat16)
            pair_real, pair_imag = lax.optimization_barrier((pair_real, pair_imag))
            spectrum = jnp.fft.fft(lax.complex(pair_real.astype(jnp.float32), pair_imag.astype(jnp.float32)), axis=-1)
            spec_real = jnp.real(spectrum).astype(jnp.bfloat16)
            spec_imag = jnp.imag(spectrum).astype(jnp.bfloat16)
            spec_real, spec_imag = lax.optimization_barrier((spec_real, spec_imag))
            full_spectrum = jnp.fft.fft2(lax.complex(spec_real.astype(jnp.float32), spec_imag.astype(jnp.float32)), axes=(1, 2))
            picked = full_spectrum[:, wrapped[1], wrapped[0], wrapped[2]] * norm_scale
            return jnp.stack([jnp.real(picked), jnp.imag(picked)]).astype(jnp.bfloat16)

        density = lax.map(one_band, valence)
        weighted = (weight[:, None, :, None] * density.astype(jnp.float32)).astype(jnp.bfloat16)
        dens_real = density[:, 0].reshape(-1, NG)
        dens_imag = density[:, 1].reshape(-1, NG)
        wgt_real = weighted[:, 0].reshape(-1, NG)
        wgt_imag = weighted[:, 1].reshape(-1, NG)
        right_side = jnp.concatenate([dens_real, dens_imag], axis=0)
        left_real = jnp.concatenate([wgt_real, wgt_imag], axis=0)
        left_imag = jnp.concatenate([wgt_imag, -wgt_real], axis=0)
        chi_real = jnp.dot(left_real.T, right_side, preferred_element_type=jnp.float32)
        chi_imag = jnp.dot(left_imag.T, right_side, preferred_element_type=jnp.float32)
        return running + jnp.stack([chi_real, chi_imag]), None

    chi_start = jnp.zeros((2, NG, NG), jnp.float32)
    chi_zero, _ = lax.scan(one_kpoint, chi_start, jnp.arange(NK, dtype=jnp.int32))
    return chi_zero
```

```python
import math

import jax
import jax.numpy as jnp
import numpy as np
from jax import lax
from jax.experimental import pallas as pl
from jax.experimental.pallas import tpu as pltpu
from jax.sharding import Mesh
from jax.sharding import PartitionSpec as P

GRID = 64
HALF = 32
NG = 2048
NOCC = 16
SLAB = 8
AXES = ("xh", "z", "c", "xl", "y")
KA = ("xh", "z", "c")
BAND = ("xl", "y")


def tables():
    pos = np.arange(GRID)
    freq = np.arange(HALF) - HALF // 2
    ang = (freq[:, None] * pos[None, :] % GRID) * (2.0 * math.pi / GRID)
    cos, sin = np.cos(ang), np.sin(ang)
    eye = np.eye(SLAB)
    ymat = np.stack([cos, sin])
    ymat = np.einsum("wgy,xu->wgxyu", ymat, eye).reshape(2 * HALF * SLAB, GRID * SLAB)
    ct, st = cos.T, sin.T
    zre = np.concatenate([ct, -st, -st, -ct], axis=0)
    zim = np.concatenate([-st, -ct, -ct, st], axis=0)
    zmat = np.zeros((4, 4 * GRID, 2, 4, HALF))
    for g in range(4):
        zmat[g, :, 0, g] = zre
        zmat[g, :, 1, g] = zim
    zmat = zmat.reshape(1024, 256)
    scale = float(GRID) ** -1.5
    xtab = np.concatenate(
        [cos.T.reshape(8, SLAB, HALF), sin.T.reshape(8, SLAB, HALF)], axis=1
    ) * scale
    hi = xtab.astype(jnp.bfloat16).astype(np.float64)
    xtab = np.concatenate([hi, xtab - hi], axis=2)
    pick = np.zeros((8, 2, 2, 2, 2, 2, NOCC, SLAB))
    for b in range(8):
        for h in range(2):
            for j in range(2):
                for c in range(2):
                    pick[b, h, j, c, h, c, 2 * b + j, :] = 1.0
    pick = pick.reshape(64, 512)
    return [np.asarray(a, np.float32).astype(jnp.bfloat16) for a in (ymat, zmat, xtab, pick)]


def density_kernel(sel, val, cond, waves, ymat, zmat, xtab, pick, out,
                   vbuf, c1, c2, pbuf, gbuf, fbuf, cosb, sinb, sems):
    copies = [
        pltpu.make_async_copy(val.at[0, sel[0, j]], vbuf.at[j], sems.at[j])
        for j in range(NOCC)
    ]
    for copy in copies:
        copy.start()
    low = lax.broadcasted_iota(jnp.int32, (512, 128), 1) < GRID
    cf = cond[...].reshape(512, 128).astype(jnp.float32)
    cr = pltpu.roll(cf, GRID, 1)
    c1[...] = jnp.where(low, cf, cr)
    c2[...] = jnp.where(low, cr, -cf)

    gx = waves[0:1, :] + HALF // 2
    hot = (lax.broadcasted_iota(jnp.int32, (2 * HALF, NG), 0) % HALF == gx)
    hot = hot.astype(jnp.float32).astype(jnp.bfloat16)
    phase = jnp.dot(xtab[...], hot, preferred_element_type=jnp.float32)
    cosb[...] = phase[:SLAB]
    sinb[...] = phase[SLAB:]

    for copy in copies:
        copy.wait()

    def y_step(p, carry):
        for q in range(2):
            v = vbuf[2 * p + q].reshape(512, 128).astype(jnp.float32)
            pair = v * c1[...] + pltpu.roll(v, GRID, 1) * c2[...]
            pbuf[:, 128 * q:128 * (q + 1)] = pair.astype(jnp.bfloat16)
        g = jnp.dot(ymat[...], pbuf[...], preferred_element_type=jnp.float32)
        g = g.reshape(2, HALF, SLAB, 256)
        g = jnp.concatenate([g[..., :128], g[..., 128:]], axis=2).astype(jnp.bfloat16)
        for w in range(2):
            for gy in range(HALF):
                row = pl.multiple_of((gy // 4) * 128 + p * 16, 16)
                lane = ((gy % 4) * 2 + w) * 128
                gbuf[pl.ds(row, 16), lane:lane + 128] = g[w, gy]
        return carry

    lax.fori_loop(0, NOCC // 2, y_step, 0)

    for n in range(4):
        f = jnp.dot(gbuf[256 * n:256 * (n + 1), :], zmat[...], preferred_element_type=jnp.float32)
        f = f.astype(jnp.bfloat16)
        for k in range(2):
            lane = (2 * n + k) * 128
            fbuf[0:128, lane:lane + 128] = f[128 * k:128 * (k + 1), :128]
            fbuf[128:256, lane:lane + 128] = f[128 * k:128 * (k + 1), 128:]

    def t_step(n, carry):
        parts = []
        for h in range(2):
            lane = pl.multiple_of(n * 256 + h * 1024, 256)
            idx = (waves[1:2, pl.ds(lane, 256)] + HALF // 2) * HALF + (
                waves[2:3, pl.ds(lane, 256)] + HALF // 2
            )
            onehot = lax.broadcasted_iota(jnp.int32, (1024, 256), 0) == idx
            onehot = onehot.astype(jnp.float32).astype(jnp.bfloat16)
            f = jnp.dot(fbuf[...], onehot, preferred_element_type=jnp.float32)
            fr = f[:128].reshape(NOCC, SLAB, 256)
            fi = f[128:].reshape(NOCC, SLAB, 256)
            cs = cosb[:, pl.ds(lane, 256)][None]
            sn = sinb[:, pl.ds(lane, 256)][None]
            parts.append((cs * fr + sn * fi).astype(jnp.bfloat16).reshape(128, 256))
            parts.append((cs * fi - sn * fr).astype(jnp.bfloat16).reshape(128, 256))
        total = jnp.dot(pick[...], jnp.concatenate(parts, axis=0), preferred_element_type=jnp.float32)
        dst = pl.multiple_of(n * 256, 256)
        out[:, :, pl.ds(dst, 256)] = total.astype(jnp.bfloat16).reshape(8, 8, 256)
        return carry

    lax.fori_loop(0, 4, t_step, 0)


def pack_kernel(band, partner, sel, val_e, cond_e, freq, recv, out):
    total = jnp.sum(recv[...].astype(jnp.float32), axis=0).astype(jnp.bfloat16).astype(jnp.float32)
    e = cond_e[partner[0], 0]
    b = band[0]
    d0 = val_e[0, sel[0, 2 * b]] - e
    d1 = val_e[0, sel[0, 2 * b + 1]] - e
    rows = lax.broadcasted_iota(jnp.int32, (8, 128), 0)
    gap = jnp.where((rows // 2) % 2 == 0, d0, d1)
    w = freq[0]
    weight = 2.0 * gap / (gap * gap + w * w) / 512.0
    for z in range(8):
        wt = weight * total[:, 128 * z:128 * (z + 1)]
        for t in range(8):
            out[z * 8 + t] = jnp.concatenate(
                [wt, total[:, 128 * t:128 * (t + 1)]], axis=0
            ).astype(jnp.bfloat16)


def chi_kernel(recv, out, buf):
    buf[...] = recv[...].astype(jnp.float32).reshape(1024, 128)

    def rows(kind, h, j, c):
        return buf[pl.ds(8 * kind + 4 * h + 2 * j + c, 64, stride=16), :]

    right = jnp.concatenate(
        [
            jnp.concatenate([rows(1, h, j, c) for c in range(2) for j in range(2)], axis=0)
            for h in range(2)
        ],
        axis=1,
    ).astype(jnp.bfloat16)
    dims = (((0,), (0,)), ((), ()))
    for h in range(2):
        re = [rows(0, h, j, 0) for j in range(2)]
        im = [rows(0, h, j, 1) for j in range(2)]
        left = jnp.concatenate(
            [jnp.concatenate(re + im, axis=0), jnp.concatenate(im + [-r for r in re], axis=0)],
            axis=1,
        ).astype(jnp.bfloat16)
        chi = lax.dot_general(left, right, dims, preferred_element_type=jnp.float32)
        chi = jnp.concatenate(
            [chi[:128].reshape(16, 8, 256), chi[128:].reshape(16, 8, 256)], axis=1
        )
        out[16 * h:16 * (h + 1)] = chi.astype(jnp.bfloat16)


def final_kernel(recv, out):
    for b in range(8):
        acc = recv[b].astype(jnp.float32)
        for s in range(1, 4):
            acc = acc + recv[8 * s + b].astype(jnp.float32)
        for h in range(2):
            lane = h * 1024 + b * 128
            out[0, :, lane:lane + 128] = acc[:8, 128 * h:128 * (h + 1)]
            out[1, :, lane:lane + 128] = acc[8:, 128 * h:128 * (h + 1)]


VM = pl.BlockSpec(memory_space=pltpu.VMEM)
SM = pl.BlockSpec(memory_space=pltpu.SMEM)


def shards(
    valence_orbitals,
    conduction_orbitals,
    valence_energy,
    conduction_energy,
    valence_select,
    shifted_index,
    wave_vectors,
    frequency,
):
    ymat, zmat, xtab, pick = tables()
    band = lax.axis_index(BAND)
    partner = lax.dynamic_slice_in_dim(shifted_index, lax.axis_index(KA), 1)
    ordered = conduction_orbitals[:, 0].at[shifted_index].get(mode="promise_in_bounds")
    cond = lax.all_to_all(ordered, KA, split_axis=0, concat_axis=0, tiled=True)
    xown = lax.dynamic_index_in_dim(jnp.asarray(xtab), band, 0, keepdims=False)
    f32, bf16 = jnp.float32, jnp.bfloat16
    partial = pl.pallas_call(
        density_kernel,
        out_shape=jax.ShapeDtypeStruct((8, 8, 1024), bf16),
        in_specs=[SM, pl.BlockSpec(memory_space=pl.ANY)] + [VM] * 6,
        out_specs=VM,
        scratch_shapes=[
            pltpu.VMEM((NOCC, GRID, SLAB, 128), bf16),
            pltpu.VMEM((512, 128), f32),
            pltpu.VMEM((512, 128), f32),
            pltpu.VMEM((512, 256), bf16),
            pltpu.VMEM((1024, 1024), bf16),
            pltpu.VMEM((256, 1024), bf16),
            pltpu.VMEM((SLAB, NG), f32),
            pltpu.VMEM((SLAB, NG), f32),
            pltpu.SemaphoreType.DMA((NOCC,)),
        ],
        name="density",
    )(valence_select, valence_orbitals, cond, wave_vectors, ymat, zmat, xown, pick)
    recv = lax.all_to_all(partial, BAND, split_axis=0, concat_axis=0, tiled=True)
    packed = pl.pallas_call(
        pack_kernel,
        out_shape=jax.ShapeDtypeStruct((64, 16, 128), bf16),
        in_specs=[SM] * 6 + [VM],
        out_specs=VM,
        name="pack",
    )(band[None], partner, valence_select, valence_energy, conduction_energy, frequency, recv)
    recv = lax.all_to_all(packed, ("z",) + BAND, split_axis=0, concat_axis=0, tiled=True)
    chi = pl.pallas_call(
        chi_kernel,
        out_shape=jax.ShapeDtypeStruct((32, 16, 256), bf16),
        in_specs=[VM],
        out_specs=VM,
        scratch_shapes=[pltpu.VMEM((1024, 128), f32)],
        name="chi",
    )(recv)
    recv = lax.all_to_all(chi, ("xh", "c") + BAND, split_axis=0, concat_axis=0, tiled=True)
    return pl.pallas_call(
        final_kernel,
        out_shape=jax.ShapeDtypeStruct((2, 8, NG), f32),
        in_specs=[VM],
        out_specs=VM,
        name="final",
    )(recv)


def solution(mesh):
    fine = Mesh(mesh.devices.reshape(2, 8, 2, 2, 4), AXES)
    in_specs = (
        P(KA, None, None, BAND, None),
        P(None, None, KA, BAND, None),
        P(KA, None),
        P(),
        P(KA, None),
        P(),
        P(),
        P(),
    )
    out_specs = P(None, AXES, None)
    return jax.shard_map(shards, mesh=fine, in_specs=in_specs, out_specs=out_specs, check_vma=False)
```

```python
import math

import jax
import jax.numpy as jnp
import numpy as np
from jax import lax
from jax.experimental import pallas as pl
from jax.experimental.pallas import tpu as pltpu
from jax.sharding import Mesh
from jax.sharding import PartitionSpec as P

GRID = 64
HALF = 32
NG = 2048
NOCC = 16
SLAB = 8
AXES = ("xh", "z", "c", "xl", "y")
KA = ("xh", "z", "c")
BAND = ("xl", "y")


def tables():
    pos = np.arange(GRID)
    freq = np.arange(HALF) - HALF // 2
    ang = (freq[:, None] * pos[None, :] % GRID) * (2.0 * math.pi / GRID)
    cos, sin = np.cos(ang), np.sin(ang)
    eye = np.eye(SLAB)
    ymat = np.stack([cos, sin])
    ymat = np.einsum("wgy,xu->wgxyu", ymat, eye).reshape(2 * HALF * SLAB, GRID * SLAB)
    ct, st = cos.T, sin.T
    zre = np.concatenate([ct, -st, -st, -ct], axis=0)
    zim = np.concatenate([-st, -ct, -ct, st], axis=0)
    zmat = np.zeros((4, 4 * GRID, 2, 4, HALF))
    for g in range(4):
        zmat[g, :, 0, g] = zre
        zmat[g, :, 1, g] = zim
    zmat = zmat.reshape(1024, 256)
    scale = float(GRID) ** -1.5
    xtab = np.concatenate(
        [cos.T.reshape(8, SLAB, HALF), sin.T.reshape(8, SLAB, HALF)], axis=1
    ) * scale
    hi = xtab.astype(jnp.bfloat16).astype(np.float64)
    xtab = np.concatenate([hi, xtab - hi], axis=2)
    pick = np.zeros((8, 2, 2, 2, 2, 2, NOCC, SLAB))
    for b in range(8):
        for h in range(2):
            for j in range(2):
                for c in range(2):
                    pick[b, h, j, c, h, c, 2 * b + j, :] = 1.0
    pick = pick.reshape(64, 512)
    return [np.asarray(a, np.float32).astype(jnp.bfloat16) for a in (ymat, zmat, xtab, pick)]


def order_kernel(shift, cond, out, idx, rows, sems):
    one = pltpu.make_async_copy(shift, idx, sems.at[0])
    two = pltpu.make_async_copy(cond, rows, sems.at[1])
    one.start()
    two.start()
    one.wait()
    two.wait()
    for k in range(32):
        out[k] = rows[idx[k], 0]


def prep_kernel(ids, sel_h, shift_h, vale_h, conde_h, freq_h, waves_h, xtab_h, phase, weight,
                sel, shift, val_e, cond_e, freq, waves, xtab, sems):
    pairs = [
        (sel_h, sel),
        (xtab_h.at[ids[1]], xtab),
        (waves_h, waves),
        (shift_h, shift),
        (vale_h, val_e),
        (conde_h, cond_e),
        (freq_h, freq),
    ]
    copies = [pltpu.make_async_copy(a, b, sems.at[i]) for i, (a, b) in enumerate(pairs)]
    for copy in copies:
        copy.start()
    for copy in copies:
        copy.wait()
    gx = waves[0:1, :] + HALF // 2
    hot = (lax.broadcasted_iota(jnp.int32, (2 * HALF, NG), 0) % HALF == gx)
    hot = hot.astype(jnp.float32).astype(jnp.bfloat16)
    phase[...] = jnp.dot(xtab[...], hot, preferred_element_type=jnp.float32)
    e = cond_e[shift[ids[0]]]
    d0 = val_e[0, sel[0, 2 * ids[1]]] - e
    d1 = val_e[0, sel[0, 2 * ids[1] + 1]] - e
    rows = lax.broadcasted_iota(jnp.int32, (8, 128), 0)
    gap = jnp.where((rows // 2) % 2 == 0, d0, d1)
    w = freq[0]
    weight[...] = 2.0 * gap / (gap * gap + w * w) / 512.0


def density_kernel(sel, val, phase, cond, waves, ymat, zmat, pick, out, vbuf, c1, c2, pbuf, gbuf, fbuf, sems):
    copies = [
        pltpu.make_async_copy(val.at[0, sel[0, j]], vbuf.at[j], sems.at[j])
        for j in range(NOCC)
    ]
    for copy in copies:
        copy.start()
    low = lax.broadcasted_iota(jnp.int32, (512, 128), 1) < GRID
    cf = cond[...].reshape(512, 128).astype(jnp.float32)
    cr = pltpu.roll(cf, GRID, 1)
    c1[...] = jnp.where(low, cf, cr).astype(jnp.bfloat16)
    c2[...] = jnp.where(low, cr, -cf).astype(jnp.bfloat16)
    for copy in copies:
        copy.wait()

    for p in range(NOCC // 2):
        for q in range(2):
            j = 2 * p + q
            v = vbuf[j].reshape(512, 128)
            pair = v * c1[...] + pltpu.roll(v, GRID, 1) * c2[...]
            pbuf[p % 2, :, 128 * q:128 * (q + 1)] = pair
        g = jnp.dot(ymat[...], pbuf[p % 2], preferred_element_type=jnp.float32)
        g = g.reshape(2, HALF, SLAB, 256)
        g = jnp.concatenate([g[..., :128], g[..., 128:]], axis=2).astype(jnp.bfloat16)
        for w in range(2):
            for gy in range(HALF):
                row = (gy // 4) * 128 + p * 16
                lane = ((gy % 4) * 2 + w) * 128
                gbuf[row:row + 16, lane:lane + 128] = g[w, gy]

    f = jnp.dot(gbuf[...], zmat[...], preferred_element_type=jnp.float32).astype(jnp.bfloat16)
    for k in range(8):
        fbuf[0:128, 128 * k:128 * (k + 1)] = f[128 * k:128 * (k + 1), :128]
        fbuf[128:256, 128 * k:128 * (k + 1)] = f[128 * k:128 * (k + 1), 128:]

    for n in range(4):
        parts = []
        for h in range(2):
            lane = n * 256 + h * 1024
            idx = (waves[1:2, lane:lane + 256] + HALF // 2) * HALF + (
                waves[2:3, lane:lane + 256] + HALF // 2
            )
            onehot = lax.broadcasted_iota(jnp.int32, (1024, 256), 0) == idx
            onehot = onehot.astype(jnp.float32).astype(jnp.bfloat16)
            f = jnp.dot(fbuf[...], onehot, preferred_element_type=jnp.float32)
            fr = f[:128].reshape(NOCC, SLAB, 256)
            fi = f[128:].reshape(NOCC, SLAB, 256)
            cs = phase[:SLAB, lane:lane + 256][None]
            sn = phase[SLAB:, lane:lane + 256][None]
            parts.append((cs * fr + sn * fi).astype(jnp.bfloat16).reshape(128, 256))
            parts.append((cs * fi - sn * fr).astype(jnp.bfloat16).reshape(128, 256))
        total = jnp.dot(pick[...], jnp.concatenate(parts, axis=0), preferred_element_type=jnp.float32)
        out[:, :, n * 256:(n + 1) * 256] = total.astype(jnp.bfloat16).reshape(8, 8, 256)


def pack_kernel(weight, recv, out):
    total = jnp.sum(recv[...].astype(jnp.float32), axis=0).astype(jnp.bfloat16).astype(jnp.float32)
    w = weight[...]
    for z in range(8):
        wt = w * total[:, 128 * z:128 * (z + 1)]
        for t in range(8):
            out[z * 8 + t] = jnp.concatenate(
                [wt, total[:, 128 * t:128 * (t + 1)]], axis=0
            ).astype(jnp.bfloat16)


def chi_kernel(recv, out, buf):
    buf[...] = recv[...].astype(jnp.float32).reshape(1024, 128)

    def rows(kind, h, j, c):
        return buf[pl.ds(8 * kind + 4 * h + 2 * j + c, 64, stride=16), :]

    right = jnp.concatenate(
        [
            jnp.concatenate([rows(1, h, j, c) for c in range(2) for j in range(2)], axis=0)
            for h in range(2)
        ],
        axis=1,
    ).astype(jnp.bfloat16)
    dims = (((0,), (0,)), ((), ()))
    for h in range(2):
        re = [rows(0, h, j, 0) for j in range(2)]
        im = [rows(0, h, j, 1) for j in range(2)]
        left = jnp.concatenate(
            [jnp.concatenate(re + im, axis=0), jnp.concatenate(im + [-r for r in re], axis=0)],
            axis=1,
        ).astype(jnp.bfloat16)
        chi = lax.dot_general(left, right, dims, preferred_element_type=jnp.float32)
        chi = jnp.concatenate(
            [chi[:128].reshape(16, 8, 256), chi[128:].reshape(16, 8, 256)], axis=1
        )
        out[16 * h:16 * (h + 1)] = chi.astype(jnp.bfloat16)


def final_kernel(recv, out):
    for b in range(8):
        acc = recv[b].astype(jnp.float32)
        for s in range(1, 4):
            acc = acc + recv[8 * s + b].astype(jnp.float32)
        for h in range(2):
            lane = h * 1024 + b * 128
            out[0, :, lane:lane + 128] = acc[:8, 128 * h:128 * (h + 1)]
            out[1, :, lane:lane + 128] = acc[8:, 128 * h:128 * (h + 1)]


VM = pl.BlockSpec(memory_space=pltpu.VMEM)
SM = pl.BlockSpec(memory_space=pltpu.SMEM)
HB = pl.BlockSpec(memory_space=pltpu.HBM)
F32, BF16 = jnp.float32, jnp.bfloat16


def call(kernel, name, shapes, specs, scratch=(), mib=4, cost=None):
    many = isinstance(shapes, list)
    structs = [
        pltpu.VMEM(s, d) if many else jax.ShapeDtypeStruct(s, d)
        for s, d in (shapes if many else [shapes])
    ]
    return pl.pallas_call(
        kernel,
        out_shape=structs if many else structs[0],
        in_specs=specs,
        out_specs=[VM] * len(structs) if many else VM,
        scratch_shapes=list(scratch),
        compiler_params=pltpu.CompilerParams(vmem_limit_bytes=mib << 20),
        cost_estimate=cost,
        name=name,
    )


def shards(
    valence_orbitals,
    conduction_orbitals,
    valence_energy,
    conduction_energy,
    valence_select,
    shifted_index,
    wave_vectors,
    frequency,
):
    ymat, zmat, xtab, pick = tables()
    ids = jnp.stack([lax.axis_index(KA), lax.axis_index(BAND)])
    ordered = call(
        order_kernel,
        "order",
        ((32, 2, SLAB, 128), BF16),
        [HB, HB],
        [
            pltpu.SMEM((32,), jnp.int32),
            pltpu.VMEM((32, 1, 2, SLAB, 128), BF16),
            pltpu.SemaphoreType.DMA((2,)),
        ],
        mib=63,
    )(shifted_index, conduction_orbitals)
    cond = lax.all_to_all(ordered, KA, split_axis=0, concat_axis=0, tiled=True)
    phase, weight = call(
        prep_kernel,
        "prep",
        [((16, NG), F32), ((8, 128), F32)],
        [SM] + [HB] * 7,
        [
            pltpu.SMEM((1, NOCC), jnp.int32),
            pltpu.SMEM((32,), jnp.int32),
            pltpu.SMEM((1, 32), F32),
            pltpu.SMEM((32,), F32),
            pltpu.SMEM((1,), F32),
            pltpu.VMEM((3, NG), jnp.int32),
            pltpu.VMEM((16, GRID), BF16),
            pltpu.SemaphoreType.DMA((7,)),
        ],
        mib=60,
        cost=pl.CostEstimate(flops=1 << 26, bytes_accessed=1 << 20, transcendentals=0),
    )(
        ids,
        valence_select,
        shifted_index,
        valence_energy,
        conduction_energy.reshape(32),
        frequency,
        wave_vectors,
        xtab,
    )
    partial = call(
        density_kernel,
        "density",
        ((8, 8, 1024), BF16),
        [SM, HB] + [VM] * 6,
        [
            pltpu.VMEM((NOCC, GRID, SLAB, 128), BF16),
            pltpu.VMEM((512, 128), BF16),
            pltpu.VMEM((512, 128), BF16),
            pltpu.VMEM((2, 512, 256), BF16),
            pltpu.VMEM((1024, 1024), BF16),
            pltpu.VMEM((256, 1024), BF16),
            pltpu.SemaphoreType.DMA((NOCC,)),
        ],
        mib=61,
    )(valence_select, valence_orbitals, phase, cond, wave_vectors, ymat, zmat, pick)
    recv = lax.all_to_all(partial, BAND, split_axis=0, concat_axis=0, tiled=True)
    packed = call(pack_kernel, "pack", ((64, 16, 128), BF16), [VM, VM])(weight, recv)
    recv = lax.all_to_all(packed, ("z",) + BAND, split_axis=0, concat_axis=0, tiled=True)
    chi = call(
        chi_kernel, "chi", ((32, 16, 256), BF16), [VM], [pltpu.VMEM((1024, 128), F32)]
    )(recv)
    recv = lax.all_to_all(chi, ("xh", "c") + BAND, split_axis=0, concat_axis=0, tiled=True)
    return call(final_kernel, "final", ((2, 8, NG), F32), [VM])(recv)


def solution(mesh):
    fine = Mesh(mesh.devices.reshape(2, 8, 2, 2, 4), AXES)
    in_specs = (
        P(KA, None, None, BAND, None),
        P(None, None, KA, BAND, None),
        P(KA, None),
        P(),
        P(KA, None),
        P(),
        P(),
        P(),
    )
    out_specs = P(None, AXES, None)
    return jax.shard_map(shards, mesh=fine, in_specs=in_specs, out_specs=out_specs, check_vma=False)
```

```python
import math

import jax
import jax.numpy as jnp
import numpy as np
from jax import lax
from jax.experimental import pallas as pl
from jax.experimental.pallas import tpu as pltpu
from jax.sharding import Mesh
from jax.sharding import PartitionSpec as P

GRID = 64
HALF = 32
NG = 2048
NOCC = 16
SLAB = 8
AXES = ("xh", "z", "c", "xl", "y")
KA = ("xh", "z", "c")
BAND = ("xl", "y")


def tables():
    pos = np.arange(GRID)
    freq = np.arange(HALF) - HALF // 2
    ang = (freq[:, None] * pos[None, :] % GRID) * (2.0 * math.pi / GRID)
    cos, sin = np.cos(ang), np.sin(ang)
    eye = np.eye(SLAB)
    ymat = np.stack([cos, sin])
    ymat = np.einsum("wgy,xu->wgxyu", ymat, eye).reshape(2 * HALF * SLAB, GRID * SLAB)
    ct, st = cos.T, sin.T
    zre = np.concatenate([ct, -st, -st, -ct], axis=0)
    zim = np.concatenate([-st, -ct, -ct, st], axis=0)
    zmat = np.zeros((4, 4 * GRID, 2, 4, HALF))
    for g in range(4):
        zmat[g, :, 0, g] = zre
        zmat[g, :, 1, g] = zim
    zmat = zmat.reshape(1024, 256)
    scale = float(GRID) ** -1.5
    xtab = np.concatenate(
        [cos.T.reshape(8, SLAB, HALF), sin.T.reshape(8, SLAB, HALF)], axis=1
    ) * scale
    hi = xtab.astype(jnp.bfloat16).astype(np.float64)
    xtab = np.concatenate([hi, xtab - hi], axis=2)
    pick = np.zeros((8, 2, 2, 2, 2, 2, NOCC, SLAB))
    for b in range(8):
        for h in range(2):
            for j in range(2):
                for c in range(2):
                    pick[b, h, j, c, h, c, 2 * b + j, :] = 1.0
    pick = pick.reshape(64, 512)
    return [np.asarray(a, np.float32).astype(jnp.bfloat16) for a in (ymat, zmat, xtab, pick)]


def order_kernel(shift, cond, out, idx, rows, sems):
    one = pltpu.make_async_copy(shift, idx, sems.at[0])
    two = pltpu.make_async_copy(cond, rows, sems.at[1])
    one.start()
    two.start()
    one.wait()
    two.wait()
    for k in range(32):
        out[k] = rows[idx[k], 0]


def prep_kernel(ids, sel_h, shift_h, vale_h, conde_h, freq_h, waves_h, xtab_h, val, ymat_h, zmat_h, phase, weight, vbuf, ymat, zmat,
                sel, shift, val_e, cond_e, freq, waves, xtab, sems, vsems):
    pairs = [
        (sel_h, sel),
        (xtab_h.at[ids[1]], xtab),
        (waves_h, waves),
        (shift_h, shift),
        (vale_h, val_e),
        (conde_h, cond_e),
        (freq_h, freq),
        (ymat_h, ymat),
        (zmat_h, zmat),
    ]
    copies = [pltpu.make_async_copy(a, b, sems.at[i]) for i, (a, b) in enumerate(pairs)]
    for copy in copies:
        copy.start()
    copies[0].wait()
    fetch = [
        pltpu.make_async_copy(val.at[0, sel[0, j]], vbuf.at[j], vsems.at[j])
        for j in range(NOCC)
    ]
    for copy in fetch:
        copy.start()
    for copy in copies[1:]:
        copy.wait()
    gx = waves[0:1, :] + HALF // 2
    hot = (lax.broadcasted_iota(jnp.int32, (2 * HALF, NG), 0) % HALF == gx)
    hot = hot.astype(jnp.float32).astype(jnp.bfloat16)
    phase[...] = jnp.dot(xtab[...], hot, preferred_element_type=jnp.float32)
    e = cond_e[shift[ids[0]]]
    d0 = val_e[0, sel[0, 2 * ids[1]]] - e
    d1 = val_e[0, sel[0, 2 * ids[1] + 1]] - e
    rows = lax.broadcasted_iota(jnp.int32, (8, 128), 0)
    gap = jnp.where((rows // 2) % 2 == 0, d0, d1)
    w = freq[0]
    weight[...] = 2.0 * gap / (gap * gap + w * w) / 512.0
    for copy in fetch:
        copy.wait()


def density_kernel(vbuf, phase, cond, waves, ymat, zmat, pick, out, c1, c2, pbuf, gbuf, fbuf):
    low = lax.broadcasted_iota(jnp.int32, (512, 128), 1) < GRID
    cf = cond[...].reshape(512, 128).astype(jnp.float32)
    cr = pltpu.roll(cf, GRID, 1)
    c1[...] = jnp.where(low, cf, cr).astype(jnp.bfloat16)
    c2[...] = jnp.where(low, cr, -cf).astype(jnp.bfloat16)

    for p in range(NOCC // 2):
        for q in range(2):
            j = 2 * p + q
            v = vbuf[j].reshape(512, 128)
            pair = v * c1[...] + pltpu.roll(v, GRID, 1) * c2[...]
            pbuf[p % 2, :, 128 * q:128 * (q + 1)] = pair
        g = jnp.dot(ymat[...], pbuf[p % 2], preferred_element_type=jnp.float32)
        g = g.reshape(2, HALF, SLAB, 256)
        g = jnp.concatenate([g[..., :128], g[..., 128:]], axis=2).astype(jnp.bfloat16)
        for w in range(2):
            for gy in range(HALF):
                row = (gy // 4) * 128 + p * 16
                lane = ((gy % 4) * 2 + w) * 128
                gbuf[row:row + 16, lane:lane + 128] = g[w, gy]

    for n in range(2):
        f = jnp.dot(
            gbuf[512 * n:512 * (n + 1), :], zmat[...], preferred_element_type=jnp.float32
        ).astype(jnp.bfloat16)
        for k in range(4):
            lane = (4 * n + k) * 128
            fbuf[0:128, lane:lane + 128] = f[128 * k:128 * (k + 1), :128]
            fbuf[128:256, lane:lane + 128] = f[128 * k:128 * (k + 1), 128:]

    for n in range(4):
        parts = []
        for h in range(2):
            lane = n * 256 + h * 1024
            idx = (waves[1:2, lane:lane + 256] + HALF // 2) * HALF + (
                waves[2:3, lane:lane + 256] + HALF // 2
            )
            onehot = lax.broadcasted_iota(jnp.int32, (1024, 256), 0) == idx
            onehot = onehot.astype(jnp.float32).astype(jnp.bfloat16)
            f = jnp.dot(fbuf[...], onehot, preferred_element_type=jnp.float32)
            fr = f[:128].reshape(NOCC, SLAB, 256)
            fi = f[128:].reshape(NOCC, SLAB, 256)
            cs = phase[:SLAB, lane:lane + 256][None]
            sn = phase[SLAB:, lane:lane + 256][None]
            parts.append((cs * fr + sn * fi).astype(jnp.bfloat16).reshape(128, 256))
            parts.append((cs * fi - sn * fr).astype(jnp.bfloat16).reshape(128, 256))
        total = jnp.dot(pick[...], jnp.concatenate(parts, axis=0), preferred_element_type=jnp.float32)
        out[:, :, n * 256:(n + 1) * 256] = total.astype(jnp.bfloat16).reshape(8, 8, 256)


def pack_kernel(weight, recv, out):
    total = jnp.sum(recv[...].astype(jnp.float32), axis=0).astype(jnp.bfloat16).astype(jnp.float32)
    w = weight[...]
    for z in range(8):
        wt = w * total[:, 128 * z:128 * (z + 1)]
        for t in range(8):
            out[z * 8 + t] = jnp.concatenate(
                [wt, total[:, 128 * t:128 * (t + 1)]], axis=0
            ).astype(jnp.bfloat16)


def chi_kernel(recv, out, buf):
    buf[...] = recv[...].astype(jnp.float32).reshape(1024, 128)

    def rows(kind, h, j, c):
        return buf[pl.ds(8 * kind + 4 * h + 2 * j + c, 64, stride=16), :]

    right = jnp.concatenate(
        [
            jnp.concatenate([rows(1, h, j, c) for c in range(2) for j in range(2)], axis=0)
            for h in range(2)
        ],
        axis=1,
    ).astype(jnp.bfloat16)
    dims = (((0,), (0,)), ((), ()))
    for h in range(2):
        re = [rows(0, h, j, 0) for j in range(2)]
        im = [rows(0, h, j, 1) for j in range(2)]
        left = jnp.concatenate(
            [jnp.concatenate(re + im, axis=0), jnp.concatenate(im + [-r for r in re], axis=0)],
            axis=1,
        ).astype(jnp.bfloat16)
        chi = lax.dot_general(left, right, dims, preferred_element_type=jnp.float32)
        chi = jnp.concatenate(
            [chi[:128].reshape(16, 8, 256), chi[128:].reshape(16, 8, 256)], axis=1
        )
        out[16 * h:16 * (h + 1)] = chi.astype(jnp.bfloat16)


def final_kernel(recv, out):
    for b in range(8):
        acc = recv[b].astype(jnp.float32)
        for s in range(1, 4):
            acc = acc + recv[8 * s + b].astype(jnp.float32)
        for h in range(2):
            lane = h * 1024 + b * 128
            out[0, :, lane:lane + 128] = acc[:8, 128 * h:128 * (h + 1)]
            out[1, :, lane:lane + 128] = acc[8:, 128 * h:128 * (h + 1)]


VM = pl.BlockSpec(memory_space=pltpu.VMEM)
SM = pl.BlockSpec(memory_space=pltpu.SMEM)
HB = pl.BlockSpec(memory_space=pltpu.HBM)
F32, BF16 = jnp.float32, jnp.bfloat16


def call(kernel, name, shapes, specs, scratch=(), mib=4, cost=None):
    many = isinstance(shapes, list)
    structs = [
        pltpu.VMEM(s, d) if many else jax.ShapeDtypeStruct(s, d)
        for s, d in (shapes if many else [shapes])
    ]
    return pl.pallas_call(
        kernel,
        out_shape=structs if many else structs[0],
        in_specs=specs,
        out_specs=[VM] * len(structs) if many else VM,
        scratch_shapes=list(scratch),
        compiler_params=pltpu.CompilerParams(vmem_limit_bytes=mib << 20),
        cost_estimate=cost,
        name=name,
    )


def shards(
    valence_orbitals,
    conduction_orbitals,
    valence_energy,
    conduction_energy,
    valence_select,
    shifted_index,
    wave_vectors,
    frequency,
):
    ymat, zmat, xtab, pick = tables()
    ids = jnp.stack([lax.axis_index(KA), lax.axis_index(BAND)])
    ordered = call(
        order_kernel,
        "order",
        ((32, 2, SLAB, 128), BF16),
        [HB, HB],
        [
            pltpu.SMEM((32,), jnp.int32),
            pltpu.VMEM((32, 1, 2, SLAB, 128), BF16),
            pltpu.SemaphoreType.DMA((2,)),
        ],
        mib=63,
    )(shifted_index, conduction_orbitals)
    cond = lax.all_to_all(ordered, KA, split_axis=0, concat_axis=0, tiled=True)
    phase, weight, vbuf, ymat, zmat = call(
        prep_kernel,
        "prep",
        [((16, NG), F32), ((8, 128), F32), ((NOCC, GRID, SLAB, 128), BF16), ((512, 512), BF16), ((1024, 256), BF16)],
        [SM] + [HB] * 10,
        [
            pltpu.SMEM((1, NOCC), jnp.int32),
            pltpu.SMEM((32,), jnp.int32),
            pltpu.SMEM((1, 32), F32),
            pltpu.SMEM((32,), F32),
            pltpu.SMEM((1,), F32),
            pltpu.VMEM((3, NG), jnp.int32),
            pltpu.VMEM((16, GRID), BF16),
            pltpu.SemaphoreType.DMA((9,)),
            pltpu.SemaphoreType.DMA((NOCC,)),
        ],
        mib=57,
        cost=pl.CostEstimate(flops=1 << 26, bytes_accessed=1 << 20, transcendentals=0),
    )(
        ids,
        valence_select,
        shifted_index,
        valence_energy,
        conduction_energy.reshape(32),
        frequency,
        wave_vectors,
        xtab,
        valence_orbitals,
        ymat,
        zmat,
    )
    partial = call(
        density_kernel,
        "density",
        ((8, 8, 1024), BF16),
        [VM] * 7,
        [
            pltpu.VMEM((512, 128), BF16),
            pltpu.VMEM((512, 128), BF16),
            pltpu.VMEM((2, 512, 256), BF16),
            pltpu.VMEM((1024, 1024), BF16),
            pltpu.VMEM((256, 1024), BF16),
        ],
        mib=8,
    )(vbuf, phase, cond, wave_vectors, ymat, zmat, pick)
    recv = lax.all_to_all(partial, BAND, split_axis=0, concat_axis=0, tiled=True)
    packed = call(pack_kernel, "pack", ((64, 16, 128), BF16), [VM, VM])(weight, recv)
    recv = lax.all_to_all(packed, ("z",) + BAND, split_axis=0, concat_axis=0, tiled=True)
    chi = call(
        chi_kernel, "chi", ((32, 16, 256), BF16), [VM], [pltpu.VMEM((1024, 128), F32)]
    )(recv)
    recv = lax.all_to_all(chi, ("xh", "c") + BAND, split_axis=0, concat_axis=0, tiled=True)
    return call(final_kernel, "final", ((2, 8, NG), F32), [VM])(recv)


def solution(mesh):
    fine = Mesh(mesh.devices.reshape(2, 8, 2, 2, 4), AXES)
    in_specs = (
        P(KA, None, None, BAND, None),
        P(None, None, KA, BAND, None),
        P(KA, None),
        P(),
        P(KA, None),
        P(),
        P(),
        P(),
    )
    out_specs = P(None, AXES, None)
    return jax.shard_map(shards, mesh=fine, in_specs=in_specs, out_specs=out_specs, check_vma=False)
```

```python
import math

import jax
import jax.numpy as jnp
import numpy as np
from jax import lax
from jax.experimental import pallas as pl
from jax.experimental.pallas import tpu as pltpu
from jax.sharding import Mesh
from jax.sharding import PartitionSpec as P

GRID = 64
HALF = 32
NG = 2048
NOCC = 16
SLAB = 8
AXES = ("xh", "z", "c", "xl", "y")
KA = ("xh", "z", "c")
BAND = ("xl", "y")


def tables():
    pos = np.arange(GRID)
    freq = np.arange(HALF) - HALF // 2
    ang = (freq[:, None] * pos[None, :] % GRID) * (2.0 * math.pi / GRID)
    cos, sin = np.cos(ang), np.sin(ang)
    eye = np.eye(SLAB)
    ymat = np.stack([cos, sin])
    ymat = np.einsum("wgy,xu->wgxyu", ymat, eye).reshape(2 * HALF * SLAB, GRID * SLAB)
    ct, st = cos.T, sin.T
    zre = np.concatenate([ct, -st, -st, -ct], axis=0)
    zim = np.concatenate([-st, -ct, -ct, st], axis=0)
    zmat = np.zeros((4, 4 * GRID, 2, 4, HALF))
    for g in range(4):
        zmat[g, :, 0, g] = zre
        zmat[g, :, 1, g] = zim
    zmat = zmat.reshape(1024, 256)
    scale = float(GRID) ** -1.5
    xtab = np.concatenate(
        [cos.T.reshape(8, SLAB, HALF), sin.T.reshape(8, SLAB, HALF)], axis=1
    ) * scale
    hi = xtab.astype(jnp.bfloat16).astype(np.float64)
    xtab = np.concatenate([hi, xtab - hi], axis=2)
    pick = np.zeros((8, 2, 2, 2, 2, 2, NOCC, SLAB))
    for b in range(8):
        for h in range(2):
            for j in range(2):
                for c in range(2):
                    pick[b, h, j, c, h, c, 2 * b + j, :] = 1.0
    pick = pick.reshape(64, 512)
    return [np.asarray(a, np.float32).astype(jnp.bfloat16) for a in (ymat, zmat, xtab, pick)]


def order_kernel(shift, cond, out, idx, rows, sems):
    one = pltpu.make_async_copy(shift, idx, sems.at[0])
    two = pltpu.make_async_copy(cond, rows, sems.at[1])
    one.start()
    two.start()
    one.wait()
    two.wait()
    for k in range(32):
        out[k] = rows[idx[k], 0]


def prep_kernel(ids, sel_h, shift_h, vale_h, conde_h, freq_h, waves_h, xtab_h, val, ymat_h, zmat_h, phase, weight, vbuf, ymat, zmat,
                sel, shift, val_e, cond_e, freq, waves, xtab, sems, vsems):
    pairs = [
        (sel_h, sel),
        (xtab_h.at[ids[1]], xtab),
        (waves_h, waves),
        (shift_h, shift),
        (vale_h, val_e),
        (conde_h, cond_e),
        (freq_h, freq),
        (ymat_h, ymat),
        (zmat_h, zmat),
    ]
    copies = [pltpu.make_async_copy(a, b, sems.at[i]) for i, (a, b) in enumerate(pairs)]
    for copy in copies:
        copy.start()
    copies[0].wait()
    fetch = [
        pltpu.make_async_copy(val.at[0, sel[0, j]], vbuf.at[j], vsems.at[j])
        for j in range(NOCC)
    ]
    for copy in fetch:
        copy.start()
    for copy in copies[1:]:
        copy.wait()
    gx = waves[0:1, :] + HALF // 2
    hot = (lax.broadcasted_iota(jnp.int32, (2 * HALF, NG), 0) % HALF == gx)
    hot = hot.astype(jnp.float32).astype(jnp.bfloat16)
    phase[...] = jnp.dot(xtab[...], hot, preferred_element_type=jnp.float32)
    e = cond_e[shift[ids[0]]]
    d0 = val_e[0, sel[0, 2 * ids[1]]] - e
    d1 = val_e[0, sel[0, 2 * ids[1] + 1]] - e
    rows = lax.broadcasted_iota(jnp.int32, (8, 128), 0)
    gap = jnp.where((rows // 2) % 2 == 0, d0, d1)
    w = freq[0]
    weight[...] = 2.0 * gap / (gap * gap + w * w) / 512.0
    for copy in fetch:
        copy.wait()


def density_kernel(vbuf, phase, cond, waves, ymat, zmat, pick, out, c1, c2, pbuf, gbuf, fbuf):
    low = lax.broadcasted_iota(jnp.int32, (512, 128), 1) < GRID
    cf = cond[...].reshape(512, 128).astype(jnp.float32)
    cr = pltpu.roll(cf, GRID, 1)
    c1[...] = jnp.where(low, cf, cr).astype(jnp.bfloat16)
    c2[...] = jnp.where(low, cr, -cf).astype(jnp.bfloat16)

    for p in range(NOCC // 2):
        for q in range(2):
            j = 2 * p + q
            v = vbuf[j].reshape(512, 128)
            pair = v * c1[...] + pltpu.roll(v, GRID, 1) * c2[...]
            pbuf[p % 2, :, 128 * q:128 * (q + 1)] = pair
        g = jnp.dot(ymat[...], pbuf[p % 2], preferred_element_type=jnp.float32)
        g = g.reshape(2, HALF, SLAB, 256)
        g = jnp.concatenate([g[..., :128], g[..., 128:]], axis=2).astype(jnp.bfloat16)
        for w in range(2):
            for gy in range(HALF):
                row = (gy // 4) * 128 + p * 16
                lane = ((gy % 4) * 2 + w) * 128
                gbuf[row:row + 16, lane:lane + 128] = g[w, gy]

    for n in range(2):
        f = jnp.dot(
            gbuf[512 * n:512 * (n + 1), :], zmat[...], preferred_element_type=jnp.float32
        ).astype(jnp.bfloat16)
        for k in range(4):
            lane = (4 * n + k) * 128
            fbuf[0:128, lane:lane + 128] = f[128 * k:128 * (k + 1), :128]
            fbuf[128:256, lane:lane + 128] = f[128 * k:128 * (k + 1), 128:]

    for n in range(4):
        parts = []
        for h in range(2):
            lane = n * 256 + h * 1024
            idx = (waves[1:2, lane:lane + 256] + HALF // 2) * HALF + (
                waves[2:3, lane:lane + 256] + HALF // 2
            )
            onehot = lax.broadcasted_iota(jnp.int32, (1024, 256), 0) == idx
            onehot = onehot.astype(jnp.float32).astype(jnp.bfloat16)
            f = jnp.dot(fbuf[...], onehot, preferred_element_type=jnp.float32)
            fr = f[:128].reshape(NOCC, SLAB, 256)
            fi = f[128:].reshape(NOCC, SLAB, 256)
            cs = phase[:SLAB, lane:lane + 256][None]
            sn = phase[SLAB:, lane:lane + 256][None]
            parts.append((cs * fr + sn * fi).astype(jnp.bfloat16).reshape(128, 256))
            parts.append((cs * fi - sn * fr).astype(jnp.bfloat16).reshape(128, 256))
        total = jnp.dot(pick[...], jnp.concatenate(parts, axis=0), preferred_element_type=jnp.float32)
        out[:, :, n * 256:(n + 1) * 256] = total.astype(jnp.bfloat16).reshape(8, 8, 256)


def pack_kernel(weight, recv, out):
    total = jnp.sum(recv[...].astype(jnp.float32), axis=0).astype(jnp.bfloat16).astype(jnp.float32)
    w = weight[...]
    for z in range(8):
        wt = w * total[:, 128 * z:128 * (z + 1)]
        for t in range(8):
            out[z * 8 + t] = jnp.concatenate(
                [wt, total[:, 128 * t:128 * (t + 1)]], axis=0
            ).astype(jnp.bfloat16)


def chi_kernel(recv, own, send, buf):
    upper = lax.axis_index("c") == 1
    buf[...] = recv[...].astype(jnp.float32).reshape(1024, 128)

    def rows(kind, h, j, c):
        return buf[pl.ds(8 * kind + 4 * h + 2 * j + c, 64, stride=16), :]

    right = jnp.concatenate(
        [
            jnp.concatenate([rows(1, h, j, c) for c in range(2) for j in range(2)], axis=0)
            for h in range(2)
        ],
        axis=1,
    ).astype(jnp.bfloat16)
    dims = (((0,), (0,)), ((), ()))
    for h in range(2):
        re = [rows(0, h, j, 0) for j in range(2)]
        im = [rows(0, h, j, 1) for j in range(2)]
        left = jnp.concatenate(
            [jnp.concatenate(re + im, axis=0), jnp.concatenate(im + [-r for r in re], axis=0)],
            axis=1,
        ).astype(jnp.bfloat16)
        chi = lax.dot_general(left, right, dims, preferred_element_type=jnp.float32)
        chi = jnp.concatenate(
            [chi[:128].reshape(16, 8, 256), chi[128:].reshape(16, 8, 256)], axis=1
        )
        low, high = chi[:8], chi[8:]
        own[8 * h:8 * (h + 1)] = jnp.where(upper, high, low).astype(jnp.bfloat16)
        send[8 * h:8 * (h + 1)] = jnp.where(upper, low, high).astype(jnp.bfloat16)


def merge_kernel(own, other, out):
    out[...] = (own[...].astype(jnp.float32) + other[...].astype(jnp.float32)).astype(jnp.bfloat16)


def final_kernel(recv, out):
    for b in range(8):
        acc = recv[b].astype(jnp.float32) + recv[8 + b].astype(jnp.float32)
        for h in range(2):
            lane = h * 1024 + b * 128
            out[0, :, lane:lane + 128] = acc[:8, 128 * h:128 * (h + 1)]
            out[1, :, lane:lane + 128] = acc[8:, 128 * h:128 * (h + 1)]


VM = pl.BlockSpec(memory_space=pltpu.VMEM)
SM = pl.BlockSpec(memory_space=pltpu.SMEM)
HB = pl.BlockSpec(memory_space=pltpu.HBM)
F32, BF16 = jnp.float32, jnp.bfloat16


def call(kernel, name, shapes, specs, scratch=(), mib=4, cost=None):
    many = isinstance(shapes, list)
    structs = [
        pltpu.VMEM(s, d) if many else jax.ShapeDtypeStruct(s, d)
        for s, d in (shapes if many else [shapes])
    ]
    return pl.pallas_call(
        kernel,
        out_shape=structs if many else structs[0],
        in_specs=specs,
        out_specs=[VM] * len(structs) if many else VM,
        scratch_shapes=list(scratch),
        compiler_params=pltpu.CompilerParams(vmem_limit_bytes=mib << 20),
        cost_estimate=cost,
        name=name,
    )


def shards(
    valence_orbitals,
    conduction_orbitals,
    valence_energy,
    conduction_energy,
    valence_select,
    shifted_index,
    wave_vectors,
    frequency,
):
    ymat, zmat, xtab, pick = tables()
    ids = jnp.stack([lax.axis_index(KA), lax.axis_index(BAND)])
    ordered = call(
        order_kernel,
        "order",
        ((32, 2, SLAB, 128), BF16),
        [HB, HB],
        [
            pltpu.SMEM((32,), jnp.int32),
            pltpu.VMEM((32, 1, 2, SLAB, 128), BF16),
            pltpu.SemaphoreType.DMA((2,)),
        ],
        mib=63,
    )(shifted_index, conduction_orbitals)
    cond = lax.all_to_all(ordered, KA, split_axis=0, concat_axis=0, tiled=True)
    phase, weight, vbuf, ymat, zmat = call(
        prep_kernel,
        "prep",
        [((16, NG), F32), ((8, 128), F32), ((NOCC, GRID, SLAB, 128), BF16), ((512, 512), BF16), ((1024, 256), BF16)],
        [SM] + [HB] * 10,
        [
            pltpu.SMEM((1, NOCC), jnp.int32),
            pltpu.SMEM((32,), jnp.int32),
            pltpu.SMEM((1, 32), F32),
            pltpu.SMEM((32,), F32),
            pltpu.SMEM((1,), F32),
            pltpu.VMEM((3, NG), jnp.int32),
            pltpu.VMEM((16, GRID), BF16),
            pltpu.SemaphoreType.DMA((9,)),
            pltpu.SemaphoreType.DMA((NOCC,)),
        ],
        mib=57,
        cost=pl.CostEstimate(flops=1 << 26, bytes_accessed=1 << 20, transcendentals=0),
    )(
        ids,
        valence_select,
        shifted_index,
        valence_energy,
        conduction_energy.reshape(32),
        frequency,
        wave_vectors,
        xtab,
        valence_orbitals,
        ymat,
        zmat,
    )
    partial = call(
        density_kernel,
        "density",
        ((8, 8, 1024), BF16),
        [VM] * 7,
        [
            pltpu.VMEM((512, 128), BF16),
            pltpu.VMEM((512, 128), BF16),
            pltpu.VMEM((2, 512, 256), BF16),
            pltpu.VMEM((1024, 1024), BF16),
            pltpu.VMEM((256, 1024), BF16),
        ],
        mib=8,
    )(vbuf, phase, cond, wave_vectors, ymat, zmat, pick)
    recv = lax.all_to_all(partial, BAND, split_axis=0, concat_axis=0, tiled=True)
    packed = call(pack_kernel, "pack", ((64, 16, 128), BF16), [VM, VM])(weight, recv)
    recv = lax.all_to_all(packed, ("z",) + BAND, split_axis=0, concat_axis=0, tiled=True)
    own, send = call(
        chi_kernel,
        "chi",
        [((16, 16, 256), BF16)] * 2,
        [VM],
        [pltpu.VMEM((1024, 128), F32)],
    )(recv)
    other = lax.ppermute(send, "c", [(0, 1), (1, 0)])
    merged = call(merge_kernel, "merge", ((16, 16, 256), BF16), [VM, VM])(own, other)
    recv = lax.all_to_all(merged, ("xh",) + BAND, split_axis=0, concat_axis=0, tiled=True)
    return call(final_kernel, "final", ((2, 8, NG), F32), [VM])(recv)


def solution(mesh):
    fine = Mesh(mesh.devices.reshape(2, 8, 2, 2, 4), AXES)
    in_specs = (
        P(KA, None, None, BAND, None),
        P(None, None, KA, BAND, None),
        P(KA, None),
        P(),
        P(KA, None),
        P(),
        P(),
        P(),
    )
    out_specs = P(None, AXES, None)
    return jax.shard_map(shards, mesh=fine, in_specs=in_specs, out_specs=out_specs, check_vma=False)
```

```python
import math

import jax
import jax.numpy as jnp
import numpy as np
from jax import lax
from jax.experimental import pallas as pl
from jax.experimental.pallas import tpu as pltpu
from jax.sharding import Mesh
from jax.sharding import PartitionSpec as P

GRID = 64
HALF = 32
NG = 2048
NOCC = 16
SLAB = 8
AXES = ("xh", "z", "c", "xl", "y")
KA = ("xh", "z", "c")
BAND = ("xl", "y")


def tables():
    pos = np.arange(GRID)
    freq = np.arange(HALF) - HALF // 2
    ang = (freq[:, None] * pos[None, :] % GRID) * (2.0 * math.pi / GRID)
    cos, sin = np.cos(ang), np.sin(ang)
    eye = np.eye(SLAB)
    ymat = np.stack([cos, sin])
    ymat = np.einsum("wgy,xu->wgxyu", ymat, eye).reshape(2 * HALF * SLAB, GRID * SLAB)
    ct, st = cos.T, sin.T
    zre = np.concatenate([ct, -st, -st, -ct], axis=0)
    zim = np.concatenate([-st, -ct, -ct, st], axis=0)
    zmat = np.zeros((4, 4 * GRID, 2, 4, HALF))
    for g in range(4):
        zmat[g, :, 0, g] = zre
        zmat[g, :, 1, g] = zim
    zmat = zmat.reshape(1024, 256)
    scale = float(GRID) ** -1.5
    xtab = np.concatenate(
        [cos.T.reshape(8, SLAB, HALF), sin.T.reshape(8, SLAB, HALF)], axis=1
    ) * scale
    hi = xtab.astype(jnp.bfloat16).astype(np.float64)
    xtab = np.concatenate([hi, xtab - hi], axis=2)
    pick = np.zeros((8, 2, 2, 2, 2, 2, NOCC, SLAB))
    for b in range(8):
        for h in range(2):
            for j in range(2):
                for c in range(2):
                    pick[b, h, j, c, h, c, 2 * b + j, :] = 1.0
    pick = pick.reshape(64, 512)
    return [np.asarray(a, np.float32).astype(jnp.bfloat16) for a in (ymat, zmat, xtab, pick)]


def order_kernel(shift, cond, out, idx, rows, sems):
    one = pltpu.make_async_copy(shift, idx, sems.at[0])
    two = pltpu.make_async_copy(cond, rows, sems.at[1])
    one.start()
    two.start()
    one.wait()
    two.wait()
    for k in range(32):
        out[k] = rows[idx[k], 0]


def prep_kernel(ids, sel_h, shift_h, vale_h, conde_h, freq_h, waves_h, xtab_h, val, ymat_h, zmat_h, phase, weight, vbuf, ymat, zmat,
                sel, shift, val_e, cond_e, freq, waves, xtab, sems, vsems):
    pairs = [
        (sel_h, sel),
        (xtab_h.at[ids[1]], xtab),
        (waves_h, waves),
        (shift_h, shift),
        (vale_h, val_e),
        (conde_h, cond_e),
        (freq_h, freq),
        (ymat_h, ymat),
        (zmat_h, zmat),
    ]
    copies = [pltpu.make_async_copy(a, b, sems.at[i]) for i, (a, b) in enumerate(pairs)]
    for copy in copies:
        copy.start()
    copies[0].wait()
    fetch = [
        pltpu.make_async_copy(val.at[0, sel[0, j]], vbuf.at[j], vsems.at[j])
        for j in range(NOCC)
    ]
    for copy in fetch:
        copy.start()
    for copy in copies[1:]:
        copy.wait()
    gx = waves[0:1, :] + HALF // 2
    hot = (lax.broadcasted_iota(jnp.int32, (2 * HALF, NG), 0) % HALF == gx)
    hot = hot.astype(jnp.float32).astype(jnp.bfloat16)
    phase[...] = jnp.dot(xtab[...], hot, preferred_element_type=jnp.float32)
    e = cond_e[shift[ids[0]]]
    d0 = val_e[0, sel[0, 2 * ids[1]]] - e
    d1 = val_e[0, sel[0, 2 * ids[1] + 1]] - e
    rows = lax.broadcasted_iota(jnp.int32, (8, 128), 0)
    gap = jnp.where((rows // 2) % 2 == 0, d0, d1)
    w = freq[0]
    weight[...] = 2.0 * gap / (gap * gap + w * w) / 512.0
    for copy in fetch:
        copy.wait()


def density_kernel(vbuf, phase, cond, waves, ymat, zmat, pick, out, c1, c2, pbuf, gbuf, fbuf):
    low = lax.broadcasted_iota(jnp.int32, (512, 128), 1) < GRID
    cf = cond[...].reshape(512, 128).astype(jnp.float32)
    cr = pltpu.roll(cf, GRID, 1)
    c1[...] = jnp.where(low, cf, cr).astype(jnp.bfloat16)
    c2[...] = jnp.where(low, cr, -cf).astype(jnp.bfloat16)

    for p in range(NOCC // 2):
        for q in range(2):
            j = 2 * p + q
            v = vbuf[j].reshape(512, 128)
            pair = v * c1[...] + pltpu.roll(v, GRID, 1) * c2[...]
            pbuf[p % 2, :, 128 * q:128 * (q + 1)] = pair
        g = jnp.dot(ymat[...], pbuf[p % 2], preferred_element_type=jnp.float32)
        g = g.reshape(2, HALF, SLAB, 256)
        g = jnp.concatenate([g[..., :128], g[..., 128:]], axis=2).astype(jnp.bfloat16)
        for w in range(2):
            for gy in range(HALF):
                row = (gy // 4) * 128 + p * 16
                lane = ((gy % 4) * 2 + w) * 128
                gbuf[row:row + 16, lane:lane + 128] = g[w, gy]

    for n in range(2):
        f = jnp.dot(
            gbuf[512 * n:512 * (n + 1), :], zmat[...], preferred_element_type=jnp.float32
        ).astype(jnp.bfloat16)
        for k in range(4):
            lane = (4 * n + k) * 128
            fbuf[0:128, lane:lane + 128] = f[128 * k:128 * (k + 1), :128]
            fbuf[128:256, lane:lane + 128] = f[128 * k:128 * (k + 1), 128:]

    for n in range(4):
        parts = []
        for h in range(2):
            lane = n * 256 + h * 1024
            idx = (waves[1:2, lane:lane + 256] + HALF // 2) * HALF + (
                waves[2:3, lane:lane + 256] + HALF // 2
            )
            onehot = lax.broadcasted_iota(jnp.int32, (1024, 256), 0) == idx
            onehot = onehot.astype(jnp.float32).astype(jnp.bfloat16)
            f = jnp.dot(fbuf[...], onehot, preferred_element_type=jnp.float32)
            fr = f[:128].reshape(NOCC, SLAB, 256)
            fi = f[128:].reshape(NOCC, SLAB, 256)
            cs = phase[:SLAB, lane:lane + 256][None]
            sn = phase[SLAB:, lane:lane + 256][None]
            parts.append((cs * fr + sn * fi).astype(jnp.bfloat16).reshape(128, 256))
            parts.append((cs * fi - sn * fr).astype(jnp.bfloat16).reshape(128, 256))
        total = jnp.dot(pick[...], jnp.concatenate(parts, axis=0), preferred_element_type=jnp.float32)
        out[:, :, n * 256:(n + 1) * 256] = total.astype(jnp.bfloat16).reshape(8, 8, 256)


def pack_kernel(weight, recv, out):
    total = jnp.sum(recv[...].astype(jnp.float32), axis=0).astype(jnp.bfloat16).astype(jnp.float32)
    w = weight[...]
    for z in range(8):
        wt = w * total[:, 128 * z:128 * (z + 1)]
        for y in range(4):
            out[z * 4 + y] = jnp.concatenate(
                [wt, total[:, 128 * y:128 * (y + 1)], total[:, 128 * y + 512:128 * y + 640]], axis=0
            ).astype(jnp.bfloat16)


def chi_kernel(recv, own, send, buf):
    upper = lax.axis_index("c") == 1
    buf[...] = recv[...].astype(jnp.float32).reshape(768, 128)

    def rows(kind, h, j, c):
        return buf[pl.ds(8 * kind + 4 * h + 2 * j + c, 32, stride=24), :]

    right = jnp.concatenate(
        [
            jnp.concatenate([rows(1 + p, h, j, c) for c in range(2) for j in range(2)], axis=0)
            for h in range(2)
            for p in range(2)
        ],
        axis=1,
    ).astype(jnp.bfloat16)
    dims = (((0,), (0,)), ((), ()))
    for h in range(2):
        re = [rows(0, h, j, 0) for j in range(2)]
        im = [rows(0, h, j, 1) for j in range(2)]
        left = jnp.concatenate(
            [jnp.concatenate(re + im, axis=0), jnp.concatenate(im + [-r for r in re], axis=0)],
            axis=1,
        ).astype(jnp.bfloat16)
        chi = lax.dot_general(left, right, dims, preferred_element_type=jnp.float32)
        chi = jnp.concatenate(
            [chi[:128].reshape(16, 8, 512), chi[128:].reshape(16, 8, 512)], axis=1
        )
        low, high = chi[:8], chi[8:]
        own[8 * h:8 * (h + 1)] = jnp.where(upper, high, low).astype(jnp.bfloat16)
        send[8 * h:8 * (h + 1)] = jnp.where(upper, low, high).astype(jnp.bfloat16)


def merge_kernel(own, other, out):
    out[...] = (own[...].astype(jnp.float32) + other[...].astype(jnp.float32)).astype(jnp.bfloat16)


def final_kernel(recv, out):
    for y in range(4):
        acc = recv[y].astype(jnp.float32)
        for s in range(1, 4):
            acc = acc + recv[4 * s + y].astype(jnp.float32)
        for h in range(2):
            for p in range(2):
                lane = h * 1024 + p * 512 + y * 128
                part = acc[:, 256 * h + 128 * p:256 * h + 128 * (p + 1)]
                out[0, :, lane:lane + 128] = part[:8]
                out[1, :, lane:lane + 128] = part[8:]


VM = pl.BlockSpec(memory_space=pltpu.VMEM)
SM = pl.BlockSpec(memory_space=pltpu.SMEM)
HB = pl.BlockSpec(memory_space=pltpu.HBM)
F32, BF16 = jnp.float32, jnp.bfloat16


def call(kernel, name, shapes, specs, scratch=(), mib=4, cost=None):
    many = isinstance(shapes, list)
    structs = [
        pltpu.VMEM(s, d) if many else jax.ShapeDtypeStruct(s, d)
        for s, d in (shapes if many else [shapes])
    ]
    return pl.pallas_call(
        kernel,
        out_shape=structs if many else structs[0],
        in_specs=specs,
        out_specs=[VM] * len(structs) if many else VM,
        scratch_shapes=list(scratch),
        compiler_params=pltpu.CompilerParams(vmem_limit_bytes=mib << 20),
        cost_estimate=cost,
        name=name,
    )


def shards(
    valence_orbitals,
    conduction_orbitals,
    valence_energy,
    conduction_energy,
    valence_select,
    shifted_index,
    wave_vectors,
    frequency,
):
    ymat, zmat, xtab, pick = tables()
    ids = jnp.stack([lax.axis_index(KA), lax.axis_index(BAND)])
    ordered = call(
        order_kernel,
        "order",
        ((32, 2, SLAB, 128), BF16),
        [HB, HB],
        [
            pltpu.SMEM((32,), jnp.int32),
            pltpu.VMEM((32, 1, 2, SLAB, 128), BF16),
            pltpu.SemaphoreType.DMA((2,)),
        ],
        mib=63,
    )(shifted_index, conduction_orbitals)
    cond = lax.all_to_all(ordered, KA, split_axis=0, concat_axis=0, tiled=True)
    phase, weight, vbuf, ymat, zmat = call(
        prep_kernel,
        "prep",
        [((16, NG), F32), ((8, 128), F32), ((NOCC, GRID, SLAB, 128), BF16), ((512, 512), BF16), ((1024, 256), BF16)],
        [SM] + [HB] * 10,
        [
            pltpu.SMEM((1, NOCC), jnp.int32),
            pltpu.SMEM((32,), jnp.int32),
            pltpu.SMEM((1, 32), F32),
            pltpu.SMEM((32,), F32),
            pltpu.SMEM((1,), F32),
            pltpu.VMEM((3, NG), jnp.int32),
            pltpu.VMEM((16, GRID), BF16),
            pltpu.SemaphoreType.DMA((9,)),
            pltpu.SemaphoreType.DMA((NOCC,)),
        ],
        mib=57,
        cost=pl.CostEstimate(flops=1 << 26, bytes_accessed=1 << 20, transcendentals=0),
    )(
        ids,
        valence_select,
        shifted_index,
        valence_energy,
        conduction_energy.reshape(32),
        frequency,
        wave_vectors,
        xtab,
        valence_orbitals,
        ymat,
        zmat,
    )
    partial = call(
        density_kernel,
        "density",
        ((8, 8, 1024), BF16),
        [VM] * 7,
        [
            pltpu.VMEM((512, 128), BF16),
            pltpu.VMEM((512, 128), BF16),
            pltpu.VMEM((2, 512, 256), BF16),
            pltpu.VMEM((1024, 1024), BF16),
            pltpu.VMEM((256, 1024), BF16),
        ],
        mib=8,
    )(vbuf, phase, cond, wave_vectors, ymat, zmat, pick)
    recv = lax.all_to_all(partial, BAND, split_axis=0, concat_axis=0, tiled=True)
    packed = call(pack_kernel, "pack", ((32, 24, 128), BF16), [VM, VM])(weight, recv)
    recv = lax.all_to_all(packed, ("z", "y"), split_axis=0, concat_axis=0, tiled=True)
    own, send = call(
        chi_kernel,
        "chi",
        [((16, 16, 512), BF16)] * 2,
        [VM],
        [pltpu.VMEM((768, 128), F32)],
    )(recv)
    other = lax.ppermute(send, "c", [(0, 1), (1, 0)])
    merged = call(merge_kernel, "merge", ((16, 16, 512), BF16), [VM, VM])(own, other)
    recv = lax.all_to_all(merged, ("xh",) + BAND, split_axis=0, concat_axis=0, tiled=True)
    return call(final_kernel, "final", ((2, 8, NG), F32), [VM])(recv)


def solution(mesh):
    fine = Mesh(mesh.devices.reshape(2, 8, 2, 2, 4), AXES)
    in_specs = (
        P(KA, None, None, BAND, None),
        P(None, None, KA, BAND, None),
        P(KA, None),
        P(),
        P(KA, None),
        P(),
        P(),
        P(),
    )
    out_specs = P(None, AXES, None)
    return jax.shard_map(shards, mesh=fine, in_specs=in_specs, out_specs=out_specs, check_vma=False)
```

```python
import math

import jax
import jax.numpy as jnp
import numpy as np
from jax import lax
from jax.experimental import pallas as pl
from jax.experimental.pallas import tpu as pltpu
from jax.sharding import Mesh
from jax.sharding import PartitionSpec as P

GRID = 64
HALF = 32
NG = 2048
NOCC = 16
SLAB = 8
AXES = ("xh", "z", "c", "xl", "y")
KA = ("xh", "z", "c")
BAND = ("xl", "y")


def tables():
    pos = np.arange(GRID)
    freq = np.arange(HALF) - HALF // 2
    ang = (freq[:, None] * pos[None, :] % GRID) * (2.0 * math.pi / GRID)
    cos, sin = np.cos(ang), np.sin(ang)
    eye = np.eye(SLAB)
    ymat = np.stack([cos, sin])
    ymat = np.einsum("wgy,xu->wgxyu", ymat, eye).reshape(2 * HALF * SLAB, GRID * SLAB)
    ct, st = cos.T, sin.T
    zre = np.concatenate([ct, -st, -st, -ct], axis=0)
    zim = np.concatenate([-st, -ct, -ct, st], axis=0)
    zmat = np.zeros((4, 4 * GRID, 2, 4, HALF))
    for g in range(4):
        zmat[g, :, 0, g] = zre
        zmat[g, :, 1, g] = zim
    zmat = zmat.reshape(1024, 256)
    scale = float(GRID) ** -1.5
    xtab = np.concatenate(
        [cos.T.reshape(8, SLAB, HALF), sin.T.reshape(8, SLAB, HALF)], axis=1
    ) * scale
    hi = xtab.astype(jnp.bfloat16).astype(np.float64)
    xtab = np.concatenate([hi, xtab - hi], axis=2)
    pick = np.zeros((8, 2, 2, 2, 2, 2, NOCC, SLAB))
    for b in range(8):
        for h in range(2):
            for j in range(2):
                for c in range(2):
                    pick[b, h, j, c, h, c, 2 * b + j, :] = 1.0
    pick = pick.reshape(64, 512)
    return [np.asarray(a, np.float32).astype(jnp.bfloat16) for a in (ymat, zmat, xtab, pick)]


def order_kernel(shift, cond, out, idx, rows, sems):
    one = pltpu.make_async_copy(shift, idx, sems.at[0])
    two = pltpu.make_async_copy(cond, rows, sems.at[1])
    one.start()
    two.start()
    one.wait()
    two.wait()
    for k in range(32):
        out[k] = rows[idx[k], 0]


def prep_kernel(ids, sel_h, shift_h, vale_h, conde_h, freq_h, waves_h, xtab_h, val, ymat_h, zmat_h, phase, weight, vbuf, ymat, zmat,
                sel, shift, val_e, cond_e, freq, waves, xtab, sems, vsems):
    pairs = [
        (sel_h, sel),
        (xtab_h.at[ids[1]], xtab),
        (waves_h, waves),
        (shift_h, shift),
        (vale_h, val_e),
        (conde_h, cond_e),
        (freq_h, freq),
        (ymat_h, ymat),
        (zmat_h, zmat),
    ]
    copies = [pltpu.make_async_copy(a, b, sems.at[i]) for i, (a, b) in enumerate(pairs)]
    for copy in copies:
        copy.start()
    copies[0].wait()
    fetch = [
        pltpu.make_async_copy(val.at[0, sel[0, j]], vbuf.at[j], vsems.at[j])
        for j in range(NOCC)
    ]
    for copy in fetch:
        copy.start()
    for copy in copies[1:]:
        copy.wait()
    gx = waves[0:1, :] + HALF // 2
    hot = (lax.broadcasted_iota(jnp.int32, (2 * HALF, NG), 0) % HALF == gx)
    hot = hot.astype(jnp.float32).astype(jnp.bfloat16)
    phase[...] = jnp.dot(xtab[...], hot, preferred_element_type=jnp.float32)
    e = cond_e[shift[ids[0]]]
    d0 = val_e[0, sel[0, 2 * ids[1]]] - e
    d1 = val_e[0, sel[0, 2 * ids[1] + 1]] - e
    rows = lax.broadcasted_iota(jnp.int32, (8, 128), 0)
    gap = jnp.where((rows // 2) % 2 == 0, d0, d1)
    w = freq[0]
    weight[...] = 2.0 * gap / (gap * gap + w * w) / 512.0
    for copy in fetch:
        copy.wait()


def density_kernel(vbuf, phase, cond, waves, ymat, zmat, pick, out, c1, c2, pbuf, gbuf, fbuf):
    low = lax.broadcasted_iota(jnp.int32, (512, 128), 1) < GRID
    cf = cond[...].reshape(512, 128).astype(jnp.float32)
    cr = pltpu.roll(cf, GRID, 1)
    c1[...] = jnp.where(low, cf, cr).astype(jnp.bfloat16)
    c2[...] = jnp.where(low, cr, -cf).astype(jnp.bfloat16)

    for p in range(NOCC // 2):
        for q in range(2):
            j = 2 * p + q
            v = vbuf[j].reshape(512, 128)
            pair = v * c1[...] + pltpu.roll(v, GRID, 1) * c2[...]
            pbuf[p, :, 128 * q:128 * (q + 1)] = pair
        g = jnp.dot(ymat[...], pbuf[p], preferred_element_type=jnp.float32)
        g = g.reshape(2, HALF, SLAB, 256)
        g = jnp.concatenate([g[..., :128], g[..., 128:]], axis=2).astype(jnp.bfloat16)
        for w in range(2):
            for gy in range(HALF):
                row = (gy // 4) * 128 + p * 16
                lane = ((gy % 4) * 2 + w) * 128
                gbuf[row:row + 16, lane:lane + 128] = g[w, gy]

    for n in range(2):
        f = jnp.dot(
            gbuf[512 * n:512 * (n + 1), :], zmat[...], preferred_element_type=jnp.float32
        ).astype(jnp.bfloat16)
        for k in range(4):
            lane = (4 * n + k) * 128
            fbuf[0:128, lane:lane + 128] = f[128 * k:128 * (k + 1), :128]
            fbuf[128:256, lane:lane + 128] = f[128 * k:128 * (k + 1), 128:]

    for n in range(4):
        parts = []
        for h in range(2):
            lane = n * 256 + h * 1024
            idx = (waves[1:2, lane:lane + 256] + HALF // 2) * HALF + (
                waves[2:3, lane:lane + 256] + HALF // 2
            )
            onehot = lax.broadcasted_iota(jnp.int32, (1024, 256), 0) == idx
            onehot = onehot.astype(jnp.float32).astype(jnp.bfloat16)
            f = jnp.dot(fbuf[...], onehot, preferred_element_type=jnp.float32)
            fr = f[:128].reshape(NOCC, SLAB, 256)
            fi = f[128:].reshape(NOCC, SLAB, 256)
            cs = phase[:SLAB, lane:lane + 256][None]
            sn = phase[SLAB:, lane:lane + 256][None]
            parts.append((cs * fr + sn * fi).astype(jnp.bfloat16).reshape(128, 256))
            parts.append((cs * fi - sn * fr).astype(jnp.bfloat16).reshape(128, 256))
        total = jnp.dot(pick[...], jnp.concatenate(parts, axis=0), preferred_element_type=jnp.float32)
        out[:, :, n * 256:(n + 1) * 256] = total.astype(jnp.bfloat16).reshape(8, 8, 256)


def pack_kernel(weight, recv, out):
    total = jnp.sum(recv[...].astype(jnp.float32), axis=0).astype(jnp.bfloat16).astype(jnp.float32)
    w = weight[...]
    for z in range(8):
        wt = w * total[:, 128 * z:128 * (z + 1)]
        for y in range(4):
            out[z * 4 + y] = jnp.concatenate(
                [wt, total[:, 128 * y:128 * (y + 1)], total[:, 128 * y + 512:128 * y + 640]], axis=0
            ).astype(jnp.bfloat16)


def chi_kernel(recv, own, send, buf):
    upper = lax.axis_index("c") == 1
    buf[...] = recv[...].astype(jnp.float32).reshape(768, 128)

    def rows(kind, h, j, c):
        return buf[pl.ds(8 * kind + 4 * h + 2 * j + c, 32, stride=24), :]

    right = jnp.concatenate(
        [
            jnp.concatenate([rows(1 + p, h, j, c) for c in range(2) for j in range(2)], axis=0)
            for h in range(2)
            for p in range(2)
        ],
        axis=1,
    ).astype(jnp.bfloat16)
    dims = (((0,), (0,)), ((), ()))
    for h in range(2):
        re = [rows(0, h, j, 0) for j in range(2)]
        im = [rows(0, h, j, 1) for j in range(2)]
        left = jnp.concatenate(
            [jnp.concatenate(re + im, axis=0), jnp.concatenate(im + [-r for r in re], axis=0)],
            axis=1,
        ).astype(jnp.bfloat16)
        chi = lax.dot_general(left, right, dims, preferred_element_type=jnp.float32)
        chi = jnp.concatenate(
            [chi[:128].reshape(16, 8, 512), chi[128:].reshape(16, 8, 512)], axis=1
        )
        low, high = chi[:8], chi[8:]
        own[8 * h:8 * (h + 1)] = jnp.where(upper, high, low).astype(jnp.bfloat16)
        send[8 * h:8 * (h + 1)] = jnp.where(upper, low, high).astype(jnp.bfloat16)


def merge_kernel(own, other, out):
    out[...] = (own[...].astype(jnp.float32) + other[...].astype(jnp.float32)).astype(jnp.bfloat16)


def final_kernel(recv, out):
    for y in range(4):
        acc = recv[y].astype(jnp.float32)
        for s in range(1, 4):
            acc = acc + recv[4 * s + y].astype(jnp.float32)
        for h in range(2):
            for p in range(2):
                lane = h * 1024 + p * 512 + y * 128
                part = acc[:, 256 * h + 128 * p:256 * h + 128 * (p + 1)]
                out[0, :, lane:lane + 128] = part[:8]
                out[1, :, lane:lane + 128] = part[8:]


VM = pl.BlockSpec(memory_space=pltpu.VMEM)
SM = pl.BlockSpec(memory_space=pltpu.SMEM)
HB = pl.BlockSpec(memory_space=pltpu.HBM)
F32, BF16 = jnp.float32, jnp.bfloat16


def call(kernel, name, shapes, specs, scratch=(), mib=4, cost=None):
    many = isinstance(shapes, list)
    structs = [
        pltpu.VMEM(s, d) if many else jax.ShapeDtypeStruct(s, d)
        for s, d in (shapes if many else [shapes])
    ]
    return pl.pallas_call(
        kernel,
        out_shape=structs if many else structs[0],
        in_specs=specs,
        out_specs=[VM] * len(structs) if many else VM,
        scratch_shapes=list(scratch),
        compiler_params=pltpu.CompilerParams(vmem_limit_bytes=mib << 20),
        cost_estimate=cost,
        name=name,
    )


def shards(
    valence_orbitals,
    conduction_orbitals,
    valence_energy,
    conduction_energy,
    valence_select,
    shifted_index,
    wave_vectors,
    frequency,
):
    ymat, zmat, xtab, pick = tables()
    ids = jnp.stack([lax.axis_index(KA), lax.axis_index(BAND)])
    ordered = call(
        order_kernel,
        "order",
        ((32, 2, SLAB, 128), BF16),
        [HB, HB],
        [
            pltpu.SMEM((32,), jnp.int32),
            pltpu.VMEM((32, 1, 2, SLAB, 128), BF16),
            pltpu.SemaphoreType.DMA((2,)),
        ],
        mib=63,
    )(shifted_index, conduction_orbitals)
    cond = lax.all_to_all(ordered, KA, split_axis=0, concat_axis=0, tiled=True)
    phase, weight, vbuf, ymat, zmat = call(
        prep_kernel,
        "prep",
        [((16, NG), F32), ((8, 128), F32), ((NOCC, GRID, SLAB, 128), BF16), ((512, 512), BF16), ((1024, 256), BF16)],
        [SM] + [HB] * 10,
        [
            pltpu.SMEM((1, NOCC), jnp.int32),
            pltpu.SMEM((32,), jnp.int32),
            pltpu.SMEM((1, 32), F32),
            pltpu.SMEM((32,), F32),
            pltpu.SMEM((1,), F32),
            pltpu.VMEM((3, NG), jnp.int32),
            pltpu.VMEM((16, GRID), BF16),
            pltpu.SemaphoreType.DMA((9,)),
            pltpu.SemaphoreType.DMA((NOCC,)),
        ],
        mib=57,
        cost=pl.CostEstimate(flops=1 << 26, bytes_accessed=1 << 20, transcendentals=0),
    )(
        ids,
        valence_select,
        shifted_index,
        valence_energy,
        conduction_energy.reshape(32),
        frequency,
        wave_vectors,
        xtab,
        valence_orbitals,
        ymat,
        zmat,
    )
    partial = call(
        density_kernel,
        "density",
        ((8, 8, 1024), BF16),
        [VM] * 7,
        [
            pltpu.VMEM((512, 128), BF16),
            pltpu.VMEM((512, 128), BF16),
            pltpu.VMEM((8, 512, 256), BF16),
            pltpu.VMEM((1024, 1024), BF16),
            pltpu.VMEM((256, 1024), BF16),
        ],
        mib=8,
    )(vbuf, phase, cond, wave_vectors, ymat, zmat, pick)
    recv = lax.all_to_all(partial, BAND, split_axis=0, concat_axis=0, tiled=True)
    packed = call(pack_kernel, "pack", ((32, 24, 128), BF16), [VM, VM])(weight, recv)
    recv = lax.all_to_all(packed, ("z", "y"), split_axis=0, concat_axis=0, tiled=True)
    own, send = call(
        chi_kernel,
        "chi",
        [((16, 16, 512), BF16)] * 2,
        [VM],
        [pltpu.VMEM((768, 128), F32)],
    )(recv)
    other = lax.ppermute(send, "c", [(0, 1), (1, 0)])
    merged = call(merge_kernel, "merge", ((16, 16, 512), BF16), [VM, VM])(own, other)
    recv = lax.all_to_all(merged, ("xh",) + BAND, split_axis=0, concat_axis=0, tiled=True)
    return call(final_kernel, "final", ((2, 8, NG), F32), [VM])(recv)


def solution(mesh):
    fine = Mesh(mesh.devices.reshape(2, 8, 2, 2, 4), AXES)
    in_specs = (
        P(KA, None, None, BAND, None),
        P(None, None, KA, BAND, None),
        P(KA, None),
        P(),
        P(KA, None),
        P(),
        P(),
        P(),
    )
    out_specs = P(None, AXES, None)
    return jax.shard_map(shards, mesh=fine, in_specs=in_specs, out_specs=out_specs, check_vma=False)
```
